32 devices in a mesh: groups: 2 (over x), blk: 8 (over z, y), dp: 2 (over core).
Axes of the slice: x: 2, y: 2, z: 4, core: 2. Of those that a mesh axis runs over, the one named last changes fastest.
Arguments:
- particles: bfloat16 [32768, 4096], P(('groups', 'blk', 'dp')), parts along dimension 0, may hold values from -44 to 44
- defocus: int32 [32768], P(('groups', 'blk', 'dp')), parts along dimension 0, may hold values from 0 to 15
- pick_dest: int32 [32768, 1], P(('groups', 'blk', 'dp')), parts along dimension 0, may hold values from 0 to 15; in each aligned block of 1024 rows (0 to 1023, 1024 to 2047, ...) at most 128 rows name the same one
- references: bfloat16 [192, 4096], P(('groups', 'blk')), parts along dimension 0, may hold values from -4 to 4
- ctf_table: float32 [32, 4096], P('groups'), parts along dimension 0, may hold values from 0.1 to 1
Outputs:
- weighted_sums: float32 [192, 4096], P(('groups', 'blk', 'dp')), parts along dimension 0
- ctf_weights: float32 [192, 4096], P(('groups', 'blk', 'dp')), parts along dimension 0
- posterior: float32 [65536, 96], P(('groups', 'blk', 'dp')), parts along dimension 0
The draws below stay inside these ranges and needn't reach their ends.
There are 2 independent parts, one for each index of `groups`. The reference program is written for one: setup_inputs(seed, part) draws one part's arguments, and reference() takes and returns one part's arrays. A program takes and returns all parts, laid end to end along the dimension named above; each array names one. Nothing has to cross between parts.
Inputs may be any that keep to these rules, and one draw needn't show every extreme that they name: `pick_dest`: of the particles that one device holds, at most 128 name any one destination, and in every draw some device sends exactly 128 to one destination.
All inputs are finite; a program needn't handle non-finite values.
Results may differ from the reference program's by a relative error of at most 0.0028.
Values may be sent and summed in bfloat16 or wider, within the bound.
A program may use at most 128 MiB of HBM per device.

```python
import math
import jax
import jax.numpy as jnp
import numpy as np
from jax import lax

PIX = 4096
NDEF = 16
SRC = 1024
DEVS = 16
KR = 96
CAPP = 128
RECV = 2048
TOTAL = 16384
N_BLK = 8
N_DP = 2


def pieces(key):
    return jax.random.split(jax.random.fold_in(key, 91), 8)


def make_refs(key_list):
    ref_rows = jnp.clip(jax.random.normal(key_list[0], (KR, PIX), jnp.float32), -4.0, 4.0)
    return ref_rows


def make_ctf(key_list):
    return jax.random.uniform(key_list[1], (NDEF, PIX), jnp.float32, minval=0.1, maxval=1.0)


def make_defocus(key_list):
    return jax.random.randint(key_list[2], (TOTAL,), 0, NDEF, dtype=jnp.int32)


def draw_references(key, part):
    return make_refs(pieces(key)).astype(jnp.bfloat16)


def draw_ctf_table(key, part):
    return make_ctf(pieces(key))


def draw_defocus(key, part):
    return make_defocus(pieces(key))


def draw_particles(key, part):
    key_list = pieces(key)
    ref_rows = make_refs(key_list)
    ctf_rows = make_ctf(key_list)[make_defocus(key_list)]
    true_class = jax.random.randint(key_list[3], (TOTAL,), 0, KR, dtype=jnp.int32)
    signal = 0.1 * ctf_rows * ref_rows[true_class]
    noise_term = jnp.clip(jax.random.normal(key_list[4], (TOTAL, PIX), jnp.float32), -5.0, 5.0)
    drawn = signal + noise_term
    return jnp.clip(drawn, -44.0, 44.0).astype(jnp.bfloat16)


def deal_out(own_key, own, number, rows, number_of, top, reach, skew):
    sequence = jax.random.permutation(own_key, number_of)
    packed, usual = load_shares(number_of, rows * top, reach, skew, True), load_shares(number_of, rows * top, reach, skew, False)
    places = jnp.arange(number_of)

    def named(lengths, turn):
        used = int((lengths > 0).sum())
        fixed = max(1, used // 4)
        passed = fixed + (places - fixed + turn * (used - fixed)) % max(1, number_of - fixed)
        return jnp.zeros((number_of,), jnp.int32).at[sequence[jnp.where(places < fixed, places, passed)]].set(jnp.asarray(lengths, jnp.int32))

    lengths = jnp.where(number % 4 == 0, named(packed, number // 4), named(usual, number - number // 4 - 1))
    mixed = jax.random.permutation(jax.random.fold_in(own, 3), number_of)
    source_of, receiver = mixed[0:number_of // 2 * 2:2], mixed[1:number_of // 2 * 2:2]
    room = jnp.minimum(lengths[source_of] - 1, reach - lengths[receiver]) // 2
    room = jnp.where((source_of == sequence[0]) | (receiver == sequence[0]) | (lengths[receiver] == 0), 0, jnp.maximum(room, 0))
    passed = jax.random.randint(jax.random.fold_in(own, 4), (number_of // 2,), 0, 1 << 20) % (room + 1)
    lengths = lengths.at[source_of].add(-passed).at[receiver].add(passed)
    labels = jnp.searchsorted(jnp.cumsum(lengths), jnp.arange(rows * top), side="right").astype(jnp.int32)
    grid = labels.reshape(top, rows).T
    grid = grid[jax.random.permutation(jax.random.fold_in(own, 1), rows)]
    turn = jax.random.randint(jax.random.fold_in(own, 2), (rows, 1), 0, top)
    return jnp.take_along_axis(grid, (jnp.arange(top)[None, :] + turn) % top, axis=1)


def load_shares(amount, total, most, slope, full):
    weights = [(1 << 20) // math.isqrt(grade ** slope) + 1 for grade in range(1, amount + 1)]
    largest = most if full else min(most, max(-(-total // amount), total * weights[0] // sum(weights)))
    least = 1 if total - largest >= amount - 1 else 0
    holding, surplus = [largest] + [least] * (amount - 1), total - largest - least * (amount - 1)
    while surplus > 0:
        candidates = [i for i in range(1, amount) if holding[i] < largest] or [i for i in range(1, amount) if holding[i] < most]
        whole, budget = sum([weights[i] for i in candidates]), surplus
        for i in candidates:
            extra = min(most - holding[i], max(1, budget * weights[i] // whole), surplus)
            holding[i] = holding[i] + extra
            surplus = surplus - extra
    return np.array(holding)


def setup_inputs(seed: int = 0, part: int = 0) -> dict:
    key_of = jax.random.split(jax.random.key(seed), 6)
    own_keys = jax.random.split(jax.random.fold_in(key_of[5], part), 6)
    particles = draw_particles(jax.random.fold_in(jax.random.fold_in(key_of[5], part), 71), part)
    defocus = draw_defocus(jax.random.fold_in(jax.random.fold_in(key_of[5], part), 71), part)
    pick_dest_keys = jax.random.split(jax.random.fold_in(own_keys[2], 1), TOTAL // SRC)
    pick_dest_turns = jax.random.permutation(jax.random.fold_in(own_keys[2], 3), TOTAL // SRC)
    pick_dest = jax.vmap(lambda own, number: deal_out(jax.random.fold_in(own_keys[2], 2), own, number, SRC, DEVS, 1, CAPP, 2))(pick_dest_keys, pick_dest_turns).reshape((TOTAL, 1))
    references = draw_references(jax.random.fold_in(jax.random.fold_in(key_of[5], part), 71), part)
    ctf_table = draw_ctf_table(jax.random.fold_in(jax.random.fold_in(key_of[5], part), 71), part)
    return dict(particles=particles, defocus=defocus, pick_dest=pick_dest, references=references, ctf_table=ctf_table)


def reference(particles, defocus, pick_dest, references, ctf_table):
    score_scale = 1.0 / math.sqrt(PIX)
    modulation = ctf_table[defocus]
    modulated = (particles.astype(jnp.float32) * modulation).astype(jnp.bfloat16)
    ctf_square = ctf_table * ctf_table
    ref_float = references.astype(jnp.float32)
    quadratic = 0.5 * jnp.dot(ctf_square, (ref_float * ref_float).T, precision=lax.Precision.HIGHEST)
    cross_term = jnp.dot(modulated, references.T, preferred_element_type=jnp.float32)
    scores = score_scale * (cross_term - quadratic[defocus])
    largest = lax.optimization_barrier(jnp.max(scores, axis=1, keepdims=True))
    exponent = jnp.exp(scores - largest)
    weights = exponent / lax.optimization_barrier(jnp.sum(exponent, axis=1, keepdims=True))
    weights_low = weights.astype(jnp.bfloat16)
    weighted_sums = jnp.dot(weights_low.T, modulated, preferred_element_type=jnp.float32)
    onehot = (defocus[:, None] == jnp.arange(NDEF, dtype=jnp.int32)[None, :]).astype(jnp.float32)
    class_sums = jnp.dot(onehot.T, weights, precision=lax.Precision.HIGHEST)
    ctf_weights = jnp.dot(class_sums.T, ctf_square, precision=lax.Precision.HIGHEST)
    device_count = N_BLK * N_DP
    dest_grid = pick_dest[:, 0].reshape(device_count, SRC)
    dest_hot = (dest_grid[:, :, None] == jnp.arange(device_count, dtype=jnp.int32)[None, None, :]).astype(jnp.int32)
    earlier = jnp.cumsum(dest_hot, axis=1) - dest_hot
    ranking = lax.optimization_barrier(jnp.sum(earlier * dest_hot, axis=2))
    source_ids = jnp.arange(device_count, dtype=jnp.int32)[:, None]
    out_row = (dest_grid * RECV + source_ids * CAPP + ranking).reshape(-1).astype(jnp.int32)
    posterior = jnp.zeros((device_count * RECV, KR), jnp.float32).at[out_row].set(weights)
    return (weighted_sums, ctf_weights, posterior)
```

```python
import functools
import math

import jax
import jax.numpy as jnp
from jax import lax
from jax.experimental import pallas as pl
from jax.experimental.pallas import tpu as pltpu
from jax.sharding import PartitionSpec as P

F32, BF16 = jnp.float32, jnp.bfloat16
NT = (((1,), (1,)), ((), ()))
HIGH = lax.Precision.HIGHEST
ROW_BLOCK, COL_BLOCK, SUM_BLOCK, PART = 256, 512, 512, 16


def split3(x):
    hi = x.astype(BF16)
    rest = x - hi.astype(F32)
    mid = rest.astype(BF16)
    low = (rest - mid.astype(F32)).astype(BF16)
    return hi, mid, low


def kernel(
    blks, dps, capacity, turned,
    part_ref, defocus_ref, dest_ref, refs_ref, ctf_ref,
    ws_ref, cw_ref, post_ref,
    mod, gath, rfloat, rlow, ctf3, hot, hot_t, score, wlow, wpad, slot,
    post_send, post_recv, pair_send, pair_own, pair_recv, stage, sum_send, sum_recv,
    cls_send, cls_own, cls_pair, cls_sum, cls_recv,
    part_sem, ag_s, ag_r, fw_s, fw_r, post_s, post_r, pair_s, pair_r, sum_s, sum_r,
    cp_s, cp_r, cs_s, cs_r,
):
    devices = blks * dps
    rows, pix = part_ref.shape
    held_refs = refs_ref.shape[0]
    kr = blks * held_refs
    krp = rlow.shape[0]
    mine = kr // devices
    ndef = ctf_ref.shape[0]
    half = pix // 2
    row_blocks, sums = rows // ROW_BLOCK, pix // SUM_BLOCK
    parts = mine * sums // PART
    blk, core = lax.axis_index("blk"), lax.axis_index("dp")
    me = blk * dps + core
    partner = {"dp": 1 - core}

    def particle_copy(r):
        span = pl.ds(pl.multiple_of(r * ROW_BLOCK, ROW_BLOCK), ROW_BLOCK)
        return pltpu.make_async_copy(part_ref.at[span], mod.at[span], part_sem.at[r])

    for r in range(row_blocks):
        particle_copy(r).start()

    barrier = pltpu.get_barrier_semaphore()

    @pl.loop(1, devices)
    def _(k):
        d = lax.rem(me + k, devices)
        pl.semaphore_signal(
            barrier, inc=1, device_id={"blk": d // dps, "dp": lax.rem(d, dps)},
            device_id_type=pl.DeviceIdType.MESH,
        )

    pl.semaphore_wait(barrier, devices - 1)

    def remote(src, dst, send, recv, device):
        return pltpu.make_async_remote_copy(
            src_ref=src, dst_ref=dst, send_sem=send, recv_sem=recv,
            device_id=device, device_id_type=pl.DeviceIdType.MESH,
        )

    my_half = pl.ds(pl.multiple_of(core * half, half), half)
    other_half = pl.ds(pl.multiple_of((1 - core) * half, half), half)

    def gather_copy(k):
        to = lax.rem(blk + k, blks)
        return remote(refs_ref.at[:, my_half], gath.at[blk, :, my_half], ag_s.at[to], ag_r.at[blk], {"blk": to})

    def gather_arrival(b):
        return remote(refs_ref.at[:, my_half], gath.at[b, :, my_half], ag_s.at[b], ag_r.at[b], {"blk": b})

    def forward_copy(b):
        return remote(gath.at[b, :, my_half], gath.at[b, :, my_half], fw_s.at[b], fw_r.at[b], partner)

    def forward_arrival(b):
        return remote(gath.at[b, :, other_half], gath.at[b, :, other_half], fw_s.at[b], fw_r.at[b], partner)

    @pl.loop(1, blks)
    def _(k):
        gather_copy(k).start()

    ctf = ctf_ref[...]
    hi, mid, low = split3(ctf)
    ctf3[...] = jnp.zeros_like(ctf3)
    ctf3[0:ndef, :] = hi
    ctf3[ndef : 2 * ndef, :] = mid
    ctf3[2 * ndef : 3 * ndef, :] = low
    lane_class = lax.broadcasted_iota(jnp.int32, (128, rows), 0)
    hot_f = jnp.where(
        (lax.rem(lane_class, ndef) == defocus_ref[...]) & (lane_class < 3 * ndef), 1.0, 0.0
    ).astype(F32)
    hot_t[...] = hot_f.astype(BF16)
    hot[...] = hot_f.T.astype(BF16)

    def modulate(r):
        span = pl.ds(pl.multiple_of(r * ROW_BLOCK, ROW_BLOCK), ROW_BLOCK)
        particle_copy(r).wait()

        @pl.loop(0, pix // COL_BLOCK)
        def _(c):
            cols = pl.ds(pl.multiple_of(c * COL_BLOCK, COL_BLOCK), COL_BLOCK)
            factor = jnp.dot(hot[span, :], ctf3[:, cols], preferred_element_type=F32)
            mod[span, cols] = (mod[span, cols].astype(F32) * factor).astype(BF16)

    @pl.loop(0, row_blocks)
    def _(r):
        modulate(r)

    before = (
        lax.broadcasted_iota(jnp.int32, (128, 128), 0)
        < lax.broadcasted_iota(jnp.int32, (128, 128), 1)
    )
    before = jnp.where(before, 1.0, 0.0).astype(BF16)
    dest_row = lax.broadcasted_iota(jnp.int32, (devices, 128), 0)
    seen = jnp.zeros((devices, 1), F32)
    for c in range(rows // 128):
        dest = dest_ref[:, c * 128 : (c + 1) * 128]
        dest_hot = jnp.where(dest_row == dest, 1.0, 0.0).astype(F32)
        earlier = jnp.dot(dest_hot.astype(BF16), before, preferred_element_type=F32) + seen
        rank = jnp.sum(earlier * dest_hot, axis=0, keepdims=True)
        slot[:, c * 128 : (c + 1) * 128] = dest * capacity + rank.astype(jnp.int32)
        seen = seen + jnp.sum(dest_hot, axis=1, keepdims=True)

    @pl.loop(1, blks)
    def _(k):
        b = lax.rem(blk + k, blks)
        gather_arrival(b).wait_recv()
        forward_copy(b).start()

    gath[blk] = refs_ref[...]

    @pl.loop(1, blks)
    def _(k):
        forward_arrival(lax.rem(blk + k, blks)).wait_recv()

    if krp > kr:
        rfloat[kr:krp, :] = jnp.zeros((krp - kr, pix), F32)
    for b in range(blks):
        rfloat[b * held_refs : (b + 1) * held_refs, :] = gath[b].astype(F32)

    c_hi, c_mid, c_low = split3(ctf_ref[...] * ctf_ref[...])
    c_parts = jnp.concatenate([c_hi.astype(F32), c_mid.astype(F32), c_low.astype(F32)], axis=0).astype(BF16)
    quad = jnp.zeros((krp, 3 * ndef), F32)
    for c in range(pix // 1024):
        cols = slice(c * 1024, (c + 1) * 1024)
        piece = rfloat[:, cols]
        rlow[:, cols] = piece.astype(BF16)
        square = piece * piece
        s_hi = square.astype(BF16)
        s_low = (square - s_hi.astype(F32)).astype(BF16)
        quad = quad + lax.dot_general(s_hi, c_parts[:, cols], NT, preferred_element_type=F32)
        quad = quad + lax.dot_general(s_low, c_parts[:, cols], NT, preferred_element_type=F32)
    quad = 0.5 * quad

    for r in range(row_blocks):
        span = slice(r * ROW_BLOCK, (r + 1) * ROW_BLOCK)
        cross = lax.dot_general(mod[span, :], rlow[...], NT, preferred_element_type=F32)
        own_quad = jnp.dot(
            quad, hot_t[0 : 3 * ndef, span].astype(F32), precision=HIGH, preferred_element_type=F32
        )
        scores = ((cross.T - own_quad) * (1.0 / math.sqrt(pix)))[0:kr]
        exponent = jnp.exp(scores - jnp.max(scores, axis=0, keepdims=True))
        weights = exponent / jnp.sum(exponent, axis=0, keepdims=True)
        score[:, span] = weights
        wlow[:, span] = weights.astype(BF16)

    def post_copy(d):
        return remote(
            post_send.at[d], post_recv.at[me], post_s.at[d], post_r.at[me],
            {"blk": d // dps, "dp": lax.rem(d, dps)},
        )

    def post_arrival(s):
        return remote(
            post_send.at[s], post_recv.at[s], post_s.at[s], post_r.at[s],
            {"blk": s // dps, "dp": lax.rem(s, dps)},
        )

    def chosen(d):
        places = lax.broadcasted_iota(jnp.int32, (capacity, rows), 0) + d * capacity
        pick = jnp.where(places == slot[...], 1.0, 0.0).astype(BF16)
        pair = (wlow[...], pick) if turned else (pick, wlow[...])
        return lax.dot_general(*pair, NT, preferred_element_type=F32).astype(BF16)

    @pl.loop(1, devices)
    def _(k):
        d = lax.rem(me + k, devices)
        post_send[d] = chosen(d)
        post_copy(d).start()

    pads = devices * 8
    line = lax.broadcasted_iota(jnp.int32, (pads, kr), 0)
    owner_core = jnp.where(line < blks * 8, 1 - core, core)
    owner_blk = lax.rem(line // 8, blks)
    within = lax.rem(line, 8)
    wanted = (owner_blk * dps + owner_core) * mine + within
    select = jnp.where(
        (wanted == lax.broadcasted_iota(jnp.int32, (pads, kr), 1)) & (within < mine), 1.0, 0.0
    ).astype(F32)
    wpad[...] = jnp.dot(select.astype(BF16), wlow[...], preferred_element_type=F32).astype(BF16)

    w_hi, w_mid, w_low = split3(score[...])
    classes = jnp.zeros((kr, 128), F32)
    one_hot = hot_t[0:ndef, :]
    one_hot = jnp.concatenate([one_hot.astype(F32), jnp.zeros((128 - ndef, rows), F32)], axis=0).astype(BF16)
    for w in (w_low, w_mid, w_hi):
        classes = classes + lax.dot_general(w, one_hot, NT, preferred_element_type=F32)
    classes = jnp.dot(select, classes, precision=HIGH, preferred_element_type=F32)
    cls_send[...] = classes[0 : blks * 8].reshape(blks, 8, 128)
    cls_own[...] = classes[blks * 8 :].reshape(blks, 8, 128)

    class_pair = remote(cls_send, cls_pair, cp_s, cp_r, partner)
    class_pair.start()

    def pair_copy(q):
        return remote(pair_send.at[q], pair_recv.at[q], pair_s.at[q], pair_r.at[q], partner)

    @pl.loop(0, sums)
    def _(q):
        cols = pl.ds(pl.multiple_of(q * SUM_BLOCK, SUM_BLOCK), SUM_BLOCK)
        total = jnp.dot(wpad[...], mod[:, cols], preferred_element_type=F32)
        pair_send[q] = total[0 : blks * 8].astype(BF16)
        pair_own[q] = total[blks * 8 :]
        pair_copy(q).start()

    def sum_copy(b, m):
        return remote(
            sum_send.at[b, m], sum_recv.at[blk, m], sum_s.at[b, m], sum_r.at[blk, m], {"blk": b}
        )

    def sum_arrival(b, m):
        return remote(sum_send.at[b, m], sum_recv.at[b, m], sum_s.at[b, m], sum_r.at[b, m], {"blk": b})

    def class_copy(b):
        return remote(cls_sum.at[b], cls_recv.at[blk], cs_s.at[b], cs_r.at[blk], {"blk": b})

    def class_arrival(b):
        return remote(cls_sum.at[b], cls_recv.at[b], cs_s.at[b], cs_r.at[b], {"blk": b})

    class_pair.wait_recv()
    cls_sum[...] = cls_own[...] + cls_pair[...]

    @pl.loop(1, blks)
    def _(k):
        class_copy(lax.rem(blk + k, blks)).start()

    sent = 0
    for q in range(sums):
        pair_copy(q).wait_recv()
        chip = pair_own[q] + pair_recv[q].astype(F32)
        stage[:, q * mine : (q + 1) * mine, :] = chip.reshape(blks, 8, SUM_BLOCK)[:, 0:mine, :]
        while (sent + 1) * PART <= (q + 1) * mine:
            sum_send[:, sent] = stage[:, sent * PART : (sent + 1) * PART, :].astype(BF16)

            @pl.loop(1, blks)
            def _(k, sent=sent):
                sum_copy(lax.rem(blk + k, blks), sent).start()

            sent += 1

    kept = chosen(me).astype(F32)
    post_ref[pl.ds(pl.multiple_of(me * capacity, capacity), capacity), :] = kept.T if turned else kept

    @pl.loop(1, devices)
    def _(k):
        s = lax.rem(me + k, devices)
        post_arrival(s).wait_recv()
        got = post_recv[s].astype(F32)
        post_ref[pl.ds(pl.multiple_of(s * capacity, capacity), capacity), :] = got.T if turned else got

    cls_recv[blk] = cls_sum[blk]

    @pl.loop(1, blks)
    def _(k):
        class_arrival(lax.rem(blk + k, blks)).wait_recv()

    totals = jnp.sum(cls_recv[...], axis=0)[:, 0:ndef]
    ctf_now = ctf_ref[...]
    cw_ref[...] = jnp.dot(totals, ctf_now * ctf_now, precision=HIGH, preferred_element_type=F32)[0:mine]

    for m in range(parts):
        lines = slice(m * PART, (m + 1) * PART)

        def add(k, acc, m=m):
            b = lax.rem(blk + k, blks)
            sum_arrival(b, m).wait_recv()
            return acc + sum_recv[b, m].astype(F32)

        stage[0, lines, :] = lax.fori_loop(1, blks, add, stage[blk, lines, :])
    for q in range(sums):
        ws_ref[:, q * SUM_BLOCK : (q + 1) * SUM_BLOCK] = stage[0, q * mine : (q + 1) * mine, :]

    class_pair.wait_send()

    @pl.loop(1, devices)
    def _(k):
        post_copy(lax.rem(me + k, devices)).wait_send()

    @pl.loop(0, sums)
    def _(q):
        pair_copy(q).wait_send()

    @pl.loop(1, blks)
    def _(k):
        b = lax.rem(blk + k, blks)
        gather_copy(k).wait_send()
        forward_copy(b).wait_send()
        class_copy(b).wait_send()
        for m in range(parts):
            sum_copy(b, m).wait_send()


def per_device(particles, defocus, pick_dest, references, ctf_table):
    rows, pix = particles.shape
    blks, dps = lax.axis_size("blk"), lax.axis_size("dp")
    devices = blks * dps
    held = references.shape[0]
    kr = held * blks
    krp = -(-kr // 128) * 128
    capacity = max(2, 2 * rows // devices)
    mine = kr // devices
    turned = kr % 128 != 0 and capacity % 128 == 0
    sums = pix // SUM_BLOCK
    parts = mine * sums // PART
    block = (kr, capacity) if turned else (capacity, kr)
    vmem = pl.BlockSpec(memory_space=pltpu.VMEM)
    dma = pltpu.SemaphoreType.DMA
    V = pltpu.VMEM
    return tuple(
        pl.pallas_call(
            functools.partial(kernel, blks, dps, capacity, turned),
            out_shape=(
                jax.ShapeDtypeStruct((mine, pix), F32),
                jax.ShapeDtypeStruct((mine, pix), F32),
                jax.ShapeDtypeStruct((devices * capacity, kr), F32),
            ),
            in_specs=[pl.BlockSpec(memory_space=pl.ANY), vmem, vmem, vmem, vmem],
            out_specs=(vmem, vmem, vmem),
            scratch_shapes=[
                V((rows, pix), BF16), V((blks, held, pix), BF16), V((krp, pix), F32), V((krp, pix), BF16),
                V((128, pix), BF16), V((rows, 128), BF16), V((128, rows), BF16),
                V((kr, rows), F32), V((kr, rows), BF16), V((devices * 8, rows), BF16), V((1, rows), jnp.int32),
                V((devices, *block), BF16), V((devices, *block), BF16),
                V((sums, blks * 8, SUM_BLOCK), BF16), V((sums, blks * 8, SUM_BLOCK), F32),
                V((sums, blks * 8, SUM_BLOCK), BF16),
                V((blks, mine * sums, SUM_BLOCK), F32),
                V((blks, parts, PART, SUM_BLOCK), BF16), V((blks, parts, PART, SUM_BLOCK), BF16),
                V((blks, 8, 128), F32), V((blks, 8, 128), F32), V((blks, 8, 128), F32),
                V((blks, 8, 128), F32), V((blks, 8, 128), F32),
                dma((rows // ROW_BLOCK,)), dma((blks,)), dma((blks,)), dma((blks,)), dma((blks,)),
                dma((devices,)), dma((devices,)), dma((sums,)), dma((sums,)),
                dma((blks, parts)), dma((blks, parts)), dma, dma, dma((blks,)), dma((blks,)),
            ],
            compiler_params=pltpu.CompilerParams(
                collective_id=0, has_side_effects=True, vmem_limit_bytes=60 * 1024 * 1024
            ),
        )(particles, defocus.reshape(1, rows), pick_dest.reshape(1, rows), references, ctf_table)
    )


def solution(mesh):
    placed = (
        P(("groups", "blk", "dp"), None),
        P(("groups", "blk", "dp")),
        P(("groups", "blk", "dp"), None),
        P(("groups", "blk"), None),
        P("groups", None),
    )
    return jax.shard_map(
        per_device,
        mesh=mesh,
        in_specs=placed,
        out_specs=(
            P(("groups", "blk", "dp"), None),
            P(("groups", "blk", "dp"), None),
            P(("groups", "blk", "dp"), None),
        ),
        check_vma=False,
    )
```
